32 devices in a mesh: seq: 8 (over y, x, core), chan: 4 (over z).
Axes of the slice: x: 2, y: 2, z: 4, core: 2. Of those that a mesh axis runs over, the one named last changes fastest.
Arguments:
- values_in: bfloat16 [4096, 1024], P(('seq', 'chan')), may hold values from -6 to 6
- gate_in: bfloat16 [4096, 1024], P(('seq', 'chan')), may hold values from -6 to 6
- gate_out: bfloat16 [4096, 1024], P(('seq', 'chan')), may hold values from -6 to 6
- cotangent: bfloat16 [4096, 1024], P(('seq', 'chan')), may hold values from -6 to 6
- filter_spectra: float32 [2, 8, 2, 512, 1024], P(None, 'seq', None, None, 'chan'), may hold values from -4 to 4, as said below
Outputs:
- output: bfloat16 [4096, 1024], P(('seq', 'chan'))
- grad_values: bfloat16 [4096, 1024], P(('seq', 'chan'))
- grad_gate_in: bfloat16 [4096, 1024], P(('seq', 'chan'))
- grad_gate_out: bfloat16 [4096, 1024], P(('seq', 'chan'))
- grad_filter: float32 [2, 8, 2, 512, 1024], P(None, 'seq', None, None, 'chan')
The draws below stay inside these ranges and needn't reach their ends.
Inputs may be any that keep to these rules, and one draw needn't show every extreme that they name: `filter_spectra`: the spectrum is that of a real filter: the value at frequency 8192 - f is the complex conjugate of the value at f, and the values at frequencies 0 and 4096 are real.
All inputs are finite; a program needn't handle non-finite values.
Results may differ from the reference program's by a relative error of at most 0.001.
Values may be sent and summed in bfloat16 or wider, within the bound.
A program may use at most 128 MiB of HBM per device.

```python
import jax
import jax.numpy as jnp
import numpy as np
from jax import lax

D = 1024
TOK_DEV = 512
SHARDS = 8
SEQ = 4096
NFFT = 8192


def layout_frequencies_drawn():
    bit_count = SHARDS.bit_length() - 1
    mirror_table = np.zeros(SHARDS, np.int64)
    for number in range(SHARDS):
        result = 0
        for bit_place in range(bit_count):
            if number >> bit_place & 1:
                result = result | 1 << bit_count - 1 - bit_place
        mirror_table[number] = result
    shard_ids = np.arange(SHARDS)[:, None, None]
    parity = np.arange(2)[None, :, None]
    column = np.arange(TOK_DEV)[None, None, :]
    frequency = 2 * mirror_table[shard_ids] + parity + 2 * SHARDS * column
    return frequency.reshape(-1)


def draw_filter_spectra(key, part):
    total = 2 * TOK_DEV * SHARDS
    key_real = jax.random.fold_in(key, 101)
    key_imag = jax.random.fold_in(key, 202)
    real_part = jnp.clip(jax.random.normal(key_real, (total, D), jnp.float32), -4.0, 4.0)
    imag_part = jnp.clip(jax.random.normal(key_imag, (total, D), jnp.float32), -4.0, 4.0)
    mirrored = (total - jnp.arange(total, dtype=jnp.int32)) % total
    herm_real = 0.5 * (real_part + jnp.take(real_part, mirrored, axis=0))
    herm_imag = 0.5 * (imag_part - jnp.take(imag_part, mirrored, axis=0))
    ordering = jnp.asarray(layout_frequencies_drawn().astype(np.int32))
    layout_real = jnp.take(herm_real, ordering, axis=0).reshape(SHARDS, 2, TOK_DEV, D)
    layout_imag = jnp.take(herm_imag, ordering, axis=0).reshape(SHARDS, 2, TOK_DEV, D)
    return jnp.stack([layout_real, layout_imag]).astype(jnp.float32)


def shard_levels(stream_key, extent, shards, least, largest):
    factor_of, own = 1.0, jax.random.fold_in(stream_key, 6)
    for position, shards_of in shards:
        heights = jnp.exp(jax.random.uniform(jax.random.fold_in(own, position), (shards_of,), jnp.float32, least / len(shards), largest / len(shards)))
        factor_of = factor_of * jnp.repeat(heights, extent[position] // shards_of).reshape([-1 if axis == position else 1 for axis in range(len(extent))])
    return factor_of


def gaussian(stream_key, dims, width, reach, pieces=(), held_as=jnp.bfloat16):
    loudness = shard_levels(stream_key, dims, pieces, -0.22, 0.18) if pieces else 1.0
    entries = jax.random.normal(stream_key, dims, jnp.float32) * width * loudness
    return jnp.minimum(jnp.maximum(entries, -reach), reach).astype(held_as)


def setup_inputs(seed: int = 0) -> dict:
    key_list = jax.random.split(jax.random.key(seed), 6)
    return {
        "values_in": gaussian(key_list[0], (SEQ, D), 1.0, 6.0, ((0, 32),)),
        "gate_in": gaussian(key_list[1], (SEQ, D), 1.0, 6.0, ((0, 32),)),
        "gate_out": gaussian(key_list[2], (SEQ, D), 1.0, 6.0, ((0, 32),)),
        "cotangent": gaussian(key_list[3], (SEQ, D), 1.0, 6.0, ((0, 32),)),
        "filter_spectra": draw_filter_spectra(jax.random.fold_in(key_list[5], 71), 0),
    }


def layout_frequencies():
    bit_count = SHARDS.bit_length() - 1
    mirror_table = np.zeros(SHARDS, np.int64)
    for number in range(SHARDS):
        result = 0
        for bit_place in range(bit_count):
            if (number >> bit_place) & 1:
                result = result | (1 << (bit_count - 1 - bit_place))
        mirror_table[number] = result
    shard_ids = np.arange(SHARDS)[:, None, None]
    parity = np.arange(2)[None, :, None]
    column = np.arange(TOK_DEV)[None, None, :]
    frequency = 2 * mirror_table[shard_ids] + parity + 2 * SHARDS * column
    return frequency.reshape(-1)


def reference(values_in, gate_in, gate_out, cotangent, filter_spectra):
    frequency = layout_frequencies()
    to_natural = jnp.asarray(np.argsort(frequency).astype(np.int32))
    to_layout = jnp.asarray(frequency.astype(np.int32))
    flat_re = filter_spectra[0].reshape(SHARDS * 2 * TOK_DEV, D)
    flat_im = filter_spectra[1].reshape(SHARDS * 2 * TOK_DEV, D)
    spectrum = lax.complex(jnp.take(flat_re, to_natural, axis=0), jnp.take(flat_im, to_natural, axis=0))
    signal = values_in.astype(jnp.float32) * gate_in.astype(jnp.float32)
    carried = cotangent.astype(jnp.float32) * gate_out.astype(jnp.float32)
    padding = ((0, SEQ), (0, 0))
    spec_signal = jnp.fft.fft(jnp.pad(signal, padding), axis=0)
    spec_carried = jnp.fft.fft(jnp.pad(carried, padding), axis=0)
    conv = jnp.real(jnp.fft.ifft(spec_signal * spectrum, axis=0))[:SEQ]
    back = jnp.real(jnp.fft.ifft(jnp.conj(spectrum) * spec_carried, axis=0))[:SEQ]
    output = (gate_out.astype(jnp.float32) * conv).astype(jnp.bfloat16)
    grad_gate_out = (cotangent.astype(jnp.float32) * conv).astype(jnp.bfloat16)
    grad_values = (back * gate_in.astype(jnp.float32)).astype(jnp.bfloat16)
    grad_gate_in = (back * values_in.astype(jnp.float32)).astype(jnp.bfloat16)
    product = jnp.conj(spec_signal) * spec_carried / NFFT
    grad_re = jnp.take(jnp.real(product), to_layout, axis=0).reshape(SHARDS, 2, TOK_DEV, D)
    grad_im = jnp.take(jnp.imag(product), to_layout, axis=0).reshape(SHARDS, 2, TOK_DEV, D)
    grad_filter = jnp.stack([grad_re, grad_im]).astype(jnp.float32)
    return output, grad_values, grad_gate_in, grad_gate_out, grad_filter
```

```python
import functools
import math

import jax
import jax.numpy as jnp
import numpy as np
from jax import lax
from jax.experimental import pallas as pl
from jax.experimental.pallas import tpu as pltpu
from jax.sharding import PartitionSpec as P

MESH = pl.DeviceIdType.MESH
ANY = pl.BlockSpec(memory_space=pl.ANY)
WHOLE = pl.BlockSpec(memory_space=pltpu.VMEM)


def mirrored(number, bits):
    out = 0
    for place in range(bits):
        out = out + ((number >> place) & 1) * (1 << (bits - 1 - place))
    return out


def meet(peers):
    barrier = pltpu.get_barrier_semaphore()
    for peer in peers:
        pl.semaphore_signal(barrier, inc=1, device_id=peer, device_id_type=MESH)
    pl.semaphore_wait(barrier, len(peers))


def gather_kernel(shards, groups, *refs):
    inputs, held = refs[:4], refs[4]
    own_sem, z_send, z_recv, s_send, s_recv = refs[5:]
    s, c = lax.axis_index("seq"), lax.axis_index("chan")
    width = inputs[0].shape[1] // groups
    bits = shards.bit_length() - 1
    meet([(s, c ^ d) for d in range(1, groups)] + [(s ^ (1 << b), c) for b in range(bits)])

    def columns(group):
        return pl.ds(pl.multiple_of(group * width, width), width)

    crossing = {}
    for d in range(1, groups):
        for a in range(4):
            crossing[d, a] = pltpu.make_async_remote_copy(
                src_ref=inputs[a].at[:, columns(c ^ d)],
                dst_ref=held.at[s, c, a],
                send_sem=z_send.at[d * 4 + a],
                recv_sem=z_recv.at[d * 4 + a],
                device_id=(s, c ^ d),
                device_id_type=MESH,
            )
            crossing[d, a].start()
    own = [
        pltpu.make_async_copy(inputs[a].at[:, columns(c)], held.at[s, c, a], own_sem.at[a])
        for a in range(4)
    ]
    for copy in own:
        copy.start()

    def arrived(d, a):
        return pltpu.make_async_remote_copy(
            src_ref=held.at[s, c ^ d, a],
            dst_ref=held.at[s, c ^ d, a],
            send_sem=z_send.at[d * 4 + a],
            recv_sem=z_recv.at[d * 4 + a],
            device_id=(s, c ^ d),
            device_id_type=MESH,
        )

    def piece(d, owner, slot, partner):
        return pltpu.make_async_remote_copy(
            src_ref=held.at[owner, c ^ d],
            dst_ref=held.at[owner, c ^ d],
            send_sem=s_send.at[d * shards + slot],
            recv_sem=s_recv.at[d * shards + slot],
            device_id=(partner, c),
            device_id_type=MESH,
        )

    far = list(range(1, bits))
    orders = [(far if d % 2 == 0 else far[::-1]) + [0] for d in range(groups)]
    reached = []
    for d in range(groups):
        masks, levels = [0], []
        for b in orders[d]:
            levels.append([(m, m ^ (1 << b), 1 << b) for m in masks])
            masks = masks + [m ^ (1 << b) for m in masks]
        reached.append(levels)
    sent = []
    for tick in range(groups + bits):
        for d in range(groups):
            level = tick - d
            if level < 0 or level > bits:
                continue
            if level == 0:
                if d == 0:
                    for copy in own:
                        copy.wait()
                else:
                    for a in range(4):
                        arrived(d, a).wait_recv()
            else:
                for m, slot, step in reached[d][level - 1]:
                    piece(d, s ^ slot, slot, s ^ step).wait_recv()
            if level < bits:
                for m, slot, step in reached[d][level]:
                    copy = piece(d, s ^ m, slot, s ^ step)
                    copy.start()
                    sent.append(copy)
    for copy in crossing.values():
        copy.wait_send()
    for copy in sent:
        copy.wait_send()


def gather(inputs, shards, groups):
    rows, channels = inputs[0].shape
    return pl.pallas_call(
        functools.partial(gather_kernel, shards, groups),
        out_shape=jax.ShapeDtypeStruct((shards, groups, 4, rows, channels // groups), inputs[0].dtype),
        in_specs=[WHOLE] * 4,
        out_specs=ANY,
        scratch_shapes=[
            pltpu.SemaphoreType.DMA((4,)),
            pltpu.SemaphoreType.DMA((groups * 4,)),
            pltpu.SemaphoreType.DMA((groups * 4,)),
            pltpu.SemaphoreType.DMA((groups * shards,)),
            pltpu.SemaphoreType.DMA((groups * shards,)),
        ],
        compiler_params=pltpu.CompilerParams(collective_id=0, has_side_effects=True),
        name="gather",
    )(*inputs)


def trade_kernel(shards, source, target, own_sem, send_sem, recv_sem):
    s, c = lax.axis_index("seq"), lax.axis_index("chan")
    meet([(s ^ j, c) for j in range(1, shards)])

    def transfer(j):
        return pltpu.make_async_remote_copy(
            src_ref=source.at[s ^ j],
            dst_ref=target.at[s],
            send_sem=send_sem.at[j],
            recv_sem=recv_sem.at[j],
            device_id=(s ^ j, c),
            device_id_type=MESH,
        )

    def landing(j):
        return pltpu.make_async_remote_copy(
            src_ref=source.at[s ^ j],
            dst_ref=target.at[s ^ j],
            send_sem=send_sem.at[j],
            recv_sem=recv_sem.at[j],
            device_id=(s ^ j, c),
            device_id_type=MESH,
        )

    for j in range(shards - 1, 0, -1):
        transfer(j).start()
    own = pltpu.make_async_copy(source.at[s], target.at[s], own_sem)
    own.start()
    own.wait()
    for j in range(1, shards):
        landing(j).wait_recv()
    for j in range(1, shards):
        transfer(j).wait_send()


def trade(block):
    shards = block.shape[0]
    return pl.pallas_call(
        functools.partial(trade_kernel, shards),
        out_shape=jax.ShapeDtypeStruct(block.shape, block.dtype),
        in_specs=[WHOLE],
        out_specs=ANY,
        scratch_shapes=[
            pltpu.SemaphoreType.DMA,
            pltpu.SemaphoreType.DMA((shards,)),
            pltpu.SemaphoreType.DMA((shards,)),
        ],
        compiler_params=pltpu.CompilerParams(collective_id=1, has_side_effects=True),
        name="trade",
    )(block)


def deliver_kernel(shards, groups, source, target, own_sem, send_sem, recv_sem):
    s, c = lax.axis_index("seq"), lax.axis_index("chan")
    peers = [(j, d) for d in range(groups - 1, -1, -1) for j in range(shards) if j or d]
    meet([(s ^ j, c ^ d) for j, d in peers])

    def transfer(j, d, landing):
        to_s, to_c = (s ^ j, c ^ d) if landing else (s, c)
        return pltpu.make_async_remote_copy(
            src_ref=source.at[s ^ j, c ^ d],
            dst_ref=target.at[to_s, to_c],
            send_sem=send_sem.at[d * shards + j],
            recv_sem=recv_sem.at[d * shards + j],
            device_id=(s ^ j, c ^ d),
            device_id_type=MESH,
        )

    for j, d in peers:
        transfer(j, d, False).start()
    own = pltpu.make_async_copy(source.at[s, c], target.at[s, c], own_sem)
    own.start()
    own.wait()
    for j, d in peers:
        transfer(j, d, True).wait_recv()
    for j, d in peers:
        transfer(j, d, False).wait_send()


def deliver(block):
    shards, groups = block.shape[:2]
    return pl.pallas_call(
        functools.partial(deliver_kernel, shards, groups),
        out_shape=jax.ShapeDtypeStruct(block.shape, block.dtype),
        in_specs=[WHOLE],
        out_specs=ANY,
        scratch_shapes=[
            pltpu.SemaphoreType.DMA,
            pltpu.SemaphoreType.DMA((shards * groups,)),
            pltpu.SemaphoreType.DMA((shards * groups,)),
        ],
        compiler_params=pltpu.CompilerParams(collective_id=2, has_side_effects=True),
        name="deliver",
    )(block)


def halves(data):
    high = data.astype(jnp.bfloat16)
    return high, (data - high.astype(jnp.float32)).astype(jnp.bfloat16)


def product(matrix, which, high, low):
    def dot(a, b):
        return jnp.dot(a, b, preferred_element_type=jnp.float32)

    return (
        dot(matrix[which], high) + dot(matrix[which], low) + dot(matrix[which + 1], high)
    )


def spectral_kernel(coef, held, turn, matrix, filt, grad, packed, work):
    shards, groups, _, rows, lanes = held.shape
    length = groups * rows
    total = 2 * length * shards
    part = rows // shards
    for g in range(groups):
        here = pl.ds(g * rows, rows)
        for sig in range(2):
            sums = [jnp.zeros((rows, lanes), jnp.float32) for _ in range(4)]
            for i in range(shards):
                left = held[i, g, 0 if sig == 0 else 3].astype(jnp.float32)
                right = held[i, g, 1 if sig == 0 else 2].astype(jnp.float32)
                value = left * right
                for k in range(4):
                    sums[k] = sums[k] + value * coef[k, i]
            for e in range(2):
                real, imag = sums[2 * e], sums[2 * e + 1]
                cos, sin = turn[e, 0, here], turn[e, 1, here]
                at = (sig * 2 + e) * 2 * lanes
                work[here, at : at + lanes] = real * cos + imag * sin
                work[here, at + lanes : at + 2 * lanes] = imag * cos - real * sin
    span = 2 * lanes
    for e in range(2):
        spectra = []
        for sig in range(2):
            at = (sig * 2 + e) * span
            high, low = halves(work[:, at : at + span])
            by_cos = product(matrix, 0, high, low)
            by_sin = product(matrix, 2, high, low)
            spectra.append(by_cos[:, :lanes] + by_sin[:, lanes:])
            spectra.append(by_cos[:, lanes:] - by_sin[:, :lanes])
        sr, si, cr, ci = spectra
        fr, fi = filt[0, 0, e], filt[1, 0, e]
        grad[0, 0, e] = (sr * cr + si * ci) * (1.0 / total)
        grad[1, 0, e] = (sr * ci - si * cr) * (1.0 / total)
        real = (sr * fr - si * fi) - (fr * ci - fi * cr)
        imag = (sr * fi + si * fr) + (fr * cr + fi * ci)
        high, low = halves(jnp.concatenate([real, imag], axis=1))
        by_cos = product(matrix, 0, high, low)
        by_sin = product(matrix, 2, high, low)
        real = by_cos[:, :lanes] - by_sin[:, lanes:]
        imag = by_cos[:, lanes:] + by_sin[:, :lanes]
        cos, sin = turn[e, 0] * (1.0 / total), turn[e, 1] * (1.0 / total)
        done = (real * cos - imag * sin, real * sin + imag * cos)
        for p in range(2):
            for k in range(shards):
                for g in range(groups):
                    at = g * rows + k * part
                    packed[k, e, p, g * part : (g + 1) * part] = done[p][at : at + part]


def spectral(coef, held, turn, matrix, filt):
    shards, groups, _, rows, width = held.shape
    lanes = 128
    length = groups * rows
    part = length // shards
    filt_block = pl.BlockSpec((2, 1, 2, length, lanes), lambda n: (0, 0, 0, 0, n))
    return pl.pallas_call(
        spectral_kernel,
        grid=(width // lanes,),
        out_shape=(
            jax.ShapeDtypeStruct(filt.shape, jnp.float32),
            jax.ShapeDtypeStruct((shards, 2, 2, part, width), jnp.float32),
        ),
        in_specs=[
            pl.BlockSpec(memory_space=pltpu.SMEM),
            pl.BlockSpec((shards, groups, 4, rows, lanes), lambda n: (0, 0, 0, 0, n)),
            pl.BlockSpec((2, 2, length, lanes), lambda n: (0, 0, 0, 0)),
            pl.BlockSpec((4, length, length), lambda n: (0, 0, 0)),
            filt_block,
        ],
        out_specs=(
            filt_block,
            pl.BlockSpec((shards, 2, 2, part, lanes), lambda n: (0, 0, 0, 0, n)),
        ),
        scratch_shapes=[pltpu.VMEM((length, 8 * lanes), jnp.float32)],
        compiler_params=pltpu.CompilerParams(vmem_limit_bytes=60 * 1024 * 1024),
        name="spectral",
    )(coef, held, turn, matrix, filt)


def rotate(value, numerator, denominator):
    numerator = numerator % denominator
    real, imag = value
    if numerator == 0:
        return value
    if 4 * numerator == denominator:
        return (-imag, real)
    angle = 2.0 * math.pi * numerator / denominator
    cos, sin = math.cos(angle), math.sin(angle)
    return (real * cos - imag * sin, real * sin + imag * cos)


def butterflies(values):
    count = len(values)
    if count == 1:
        return values
    even, odd = butterflies(values[0::2]), butterflies(values[1::2])
    out = [None] * count
    for k in range(count // 2):
        turned = rotate(odd[k], k, count)
        out[k] = (even[k][0] + turned[0], even[k][1] + turned[1])
        out[k + count // 2] = (even[k][0] - turned[0], even[k][1] - turned[1])
    return out


def finish_kernel(pieces, gates, result):
    shards, groups, _, part, width = gates.shape
    bits = shards.bit_length() - 1
    for g in range(groups):
        rows = slice(g * part, (g + 1) * part)
        ladders = []
        for e in range(2):
            order = [mirrored(q, bits) for q in range(shards)]
            ladders.append(
                butterflies([(pieces[r, e, 0, rows], pieces[r, e, 1, rows]) for r in order])
            )
        for i in range(shards):
            odd = rotate(ladders[1][i], i, 2 * shards)
            conv = ladders[0][i][0] + odd[0]
            back = ladders[0][i][1] + odd[1]
            value = gates[i, g, 0].astype(jnp.float32)
            gate_in = gates[i, g, 1].astype(jnp.float32)
            gate_out = gates[i, g, 2].astype(jnp.float32)
            incoming = gates[i, g, 3].astype(jnp.float32)
            result[i, g, 0] = (gate_out * conv).astype(jnp.bfloat16)
            result[i, g, 1] = (back * gate_in).astype(jnp.bfloat16)
            result[i, g, 2] = (back * value).astype(jnp.bfloat16)
            result[i, g, 3] = (incoming * conv).astype(jnp.bfloat16)


def finish(pieces, gates):
    shards, groups, _, part, width = gates.shape
    lanes = 128
    gates_block = pl.BlockSpec((shards, groups, 4, part, lanes), lambda n: (0, 0, 0, 0, n))
    return pl.pallas_call(
        finish_kernel,
        grid=(width // lanes,),
        out_shape=jax.ShapeDtypeStruct(gates.shape, jnp.bfloat16),
        in_specs=[
            pl.BlockSpec((shards, 2, 2, groups * part, lanes), lambda n: (0, 0, 0, 0, n)),
            gates_block,
        ],
        out_specs=gates_block,
        name="finish",
    )(pieces, gates)


def transform_matrix(length):
    counter = np.arange(length)
    angle = 2.0 * math.pi * (np.outer(counter, counter) % length) / length
    out = []
    for table in (np.cos(angle), np.sin(angle)):
        high = table.astype(jnp.bfloat16)
        out += [high, (table - high.astype(np.float64)).astype(jnp.bfloat16)]
    return jnp.asarray(np.stack(out))


def on_device(shards, groups, values_in, gate_in, gate_out, cotangent, filter_spectra):
    rows = values_in.shape[0]
    length = rows * groups
    total = 2 * length * shards
    index = lax.axis_index("seq")
    residue = 2 * mirrored(index, shards.bit_length() - 1) + jnp.arange(2, dtype=jnp.int32)
    shard = jnp.arange(shards, dtype=jnp.int32)
    angle = (2.0 * math.pi / (2 * shards)) * (
        residue[:, None] * shard[None, :] % (2 * shards)
    ).astype(jnp.float32)
    coef = jnp.stack([jnp.cos(angle), -jnp.sin(angle)], axis=1).reshape(4, shards)
    position = jnp.arange(length, dtype=jnp.int32)
    angle = (2.0 * math.pi / total) * (residue[:, None] * position[None, :] % total).astype(
        jnp.float32
    )
    turn = jnp.stack([jnp.cos(angle), jnp.sin(angle)], axis=1)
    turn = jnp.broadcast_to(turn[..., None], (2, 2, length, 128))

    held = gather((values_in, gate_in, gate_out, cotangent), shards, groups)
    grad_filter, packed = spectral(coef, held, turn, transform_matrix(length), filter_spectra)
    part = rows // shards
    gates = lax.dynamic_slice_in_dim(held, index * part, part, axis=3)
    result = deliver(finish(trade(packed), gates))
    outs = [
        result[:, :, a].transpose(0, 2, 1, 3).reshape(rows, values_in.shape[1]) for a in range(4)
    ]
    return (outs[0], outs[1], outs[2], outs[3], grad_filter)


def solution(mesh):
    tokens = P(("seq", "chan"), None)
    spectrum = P(None, "seq", None, None, "chan")
    return jax.shard_map(
        functools.partial(on_device, mesh.shape["seq"], mesh.shape["chan"]),
        mesh=mesh,
        in_specs=(tokens, tokens, tokens, tokens, spectrum),
        out_specs=(tokens, tokens, tokens, tokens, spectrum),
        check_vma=False,
    )
```

```python
import functools
import math

import jax
import jax.numpy as jnp
import numpy as np
from jax import lax
from jax.experimental import pallas as pl
from jax.experimental.pallas import tpu as pltpu
from jax.sharding import PartitionSpec as P

MESH = pl.DeviceIdType.MESH
ANY = pl.BlockSpec(memory_space=pl.ANY)
WHOLE = pl.BlockSpec(memory_space=pltpu.VMEM)


def mirrored(number, bits):
    out = 0
    for place in range(bits):
        out = out + ((number >> place) & 1) * (1 << (bits - 1 - place))
    return out


def meet(peers):
    barrier = pltpu.get_barrier_semaphore()
    for peer in peers:
        pl.semaphore_signal(barrier, inc=1, device_id=peer, device_id_type=MESH)
    pl.semaphore_wait(barrier, len(peers))


def gather_kernel(shards, groups, *refs):
    inputs, filt, held, other = refs[:4], refs[4], refs[5], refs[6]
    own_sem, z_send, z_recv, s_send, s_recv, f_send, f_recv = refs[7:]
    s, c = lax.axis_index("seq"), lax.axis_index("chan")
    half = s % 2
    pair = s // 2
    width = inputs[0].shape[1] // groups
    lanes = width // 2
    bits = shards.bit_length() - 1
    near = [(d, e) for d in range(groups) for e in range(2) if d or e]
    meet([(s ^ e, c ^ d) for d, e in near] + [(s ^ (1 << b), c) for b in range(1, bits)])

    def columns(group, side):
        return pl.ds(pl.multiple_of(group * width + side * lanes, lanes), lanes)

    def cross(d, e, a, landing):
        at = (d * 2 + e) * 4 + a
        return pltpu.make_async_remote_copy(
            src_ref=inputs[a].at[:, columns(c ^ d, half ^ e)],
            dst_ref=held.at[s ^ e, c ^ d, a] if landing else held.at[s, c, a],
            send_sem=z_send.at[at],
            recv_sem=z_recv.at[at],
            device_id=(s ^ e, c ^ d),
            device_id_type=MESH,
        )

    for d, e in near:
        for a in range(4):
            cross(d, e, a, False).start()
    own = [
        pltpu.make_async_copy(inputs[a].at[:, columns(c, half)], held.at[s, c, a], own_sem.at[a])
        for a in range(4)
    ]
    for copy in own:
        copy.start()
    swap = pltpu.make_async_remote_copy(
        src_ref=filt.at[:, :, :, :, columns(0, half ^ 1)],
        dst_ref=other,
        send_sem=f_send,
        recv_sem=f_recv,
        device_id=(s ^ 1, c),
        device_id_type=MESH,
    )

    def piece(d, owner, slot, partner):
        place = held.at[pl.ds(owner * 2, 2), c ^ d]
        return pltpu.make_async_remote_copy(
            src_ref=place,
            dst_ref=place,
            send_sem=s_send.at[d * (shards // 2) + slot],
            recv_sem=s_recv.at[d * (shards // 2) + slot],
            device_id=(partner * 2 + half, c),
            device_id_type=MESH,
        )

    far = list(range(bits - 1))
    sent, landed = [], []
    for tick in range(groups + bits):
        for d in range(groups):
            order = far if d % 2 == 0 else far[::-1]
            depth = tick - d
            for mask in range(shards // 2):
                if bin(mask).count("1") != depth:
                    continue
                last = max([order.index(b) for b in far if mask >> b & 1], default=-1)
                later = order[last + 1 :]
                if not later:
                    landed.append((d, mask))
                    continue
                if mask:
                    piece(d, pair ^ mask, mask, pair).wait_recv()
                else:
                    for e in range(2):
                        for a in range(4):
                            if d or e:
                                cross(d, e, a, True).wait_recv()
                            else:
                                own[a].wait()
                for b in later:
                    copy = piece(d, pair ^ mask, mask ^ (1 << b), pair ^ (1 << b))
                    copy.start()
                    sent.append(copy)
        if tick == 0:
            swap.start()
    for d, mask in landed:
        piece(d, pair ^ mask, mask, pair).wait_recv()
    swap.wait_recv()
    for d, e in near:
        for a in range(4):
            cross(d, e, a, False).wait_send()
    for copy in sent:
        copy.wait_send()
    swap.wait_send()


def gather(inputs, filt, shards, groups):
    rows, channels = inputs[0].shape
    lanes = channels // groups // 2
    return pl.pallas_call(
        functools.partial(gather_kernel, shards, groups),
        out_shape=(
            jax.ShapeDtypeStruct((shards, groups, 4, rows, lanes), inputs[0].dtype),
            jax.ShapeDtypeStruct(filt.shape[:-1] + (lanes,), filt.dtype),
        ),
        in_specs=[WHOLE] * 4 + [ANY],
        out_specs=(ANY, ANY),
        scratch_shapes=[
            pltpu.SemaphoreType.DMA((4,)),
            pltpu.SemaphoreType.DMA((groups * 8,)),
            pltpu.SemaphoreType.DMA((groups * 8,)),
            pltpu.SemaphoreType.DMA((groups * shards // 2,)),
            pltpu.SemaphoreType.DMA((groups * shards // 2,)),
            pltpu.SemaphoreType.DMA,
            pltpu.SemaphoreType.DMA,
        ],
        compiler_params=pltpu.CompilerParams(collective_id=0, has_side_effects=True),
        name="gather",
    )(*inputs, filt)


def trade_kernel(shards, source, grad, target, other, own_sem, send_sem, recv_sem):
    s, c = lax.axis_index("seq"), lax.axis_index("chan")
    pairs = shards // 2
    pair, half = s // 2, s % 2
    meet([((pair ^ j) * 2 + half, c) for j in range(1, pairs)] + [(s ^ 1, c)])

    def transfer(j, landing):
        return pltpu.make_async_remote_copy(
            src_ref=source.at[pair ^ j],
            dst_ref=target.at[pair ^ j] if landing else target.at[pair],
            send_sem=send_sem.at[j],
            recv_sem=recv_sem.at[j],
            device_id=((pair ^ j) * 2 + half, c),
            device_id_type=MESH,
        )

    swap = pltpu.make_async_remote_copy(
        src_ref=grad,
        dst_ref=other,
        send_sem=send_sem.at[0],
        recv_sem=recv_sem.at[0],
        device_id=(s ^ 1, c),
        device_id_type=MESH,
    )
    for j in range(pairs - 1, 0, -1):
        transfer(j, False).start()
    swap.start()
    own = pltpu.make_async_copy(source.at[pair], target.at[pair], own_sem)
    own.start()
    own.wait()
    swap.wait_recv()
    for j in range(1, pairs):
        transfer(j, True).wait_recv()
    for j in range(1, pairs):
        transfer(j, False).wait_send()
    swap.wait_send()


def trade(block, grad):
    pairs = block.shape[0]
    return pl.pallas_call(
        functools.partial(trade_kernel, 2 * pairs),
        out_shape=(
            jax.ShapeDtypeStruct(block.shape, block.dtype),
            jax.ShapeDtypeStruct(grad.shape, grad.dtype),
        ),
        in_specs=[WHOLE, ANY],
        out_specs=(ANY, ANY),
        scratch_shapes=[
            pltpu.SemaphoreType.DMA,
            pltpu.SemaphoreType.DMA((pairs,)),
            pltpu.SemaphoreType.DMA((pairs,)),
        ],
        compiler_params=pltpu.CompilerParams(collective_id=1, has_side_effects=True),
        name="trade",
    )(block, grad)


def deliver_kernel(shards, groups, source, target, own_sem, send_sem, recv_sem):
    s, c = lax.axis_index("seq"), lax.axis_index("chan")
    peers = [(j, d) for d in range(groups - 1, -1, -1) for j in range(shards) if j or d]
    meet([(s ^ j, c ^ d) for j, d in peers])

    def transfer(j, d, landing):
        to_s, to_c = (s ^ j, c ^ d) if landing else (s, c)
        return pltpu.make_async_remote_copy(
            src_ref=source.at[s ^ j, c ^ d],
            dst_ref=target.at[to_s, to_c],
            send_sem=send_sem.at[d * shards + j],
            recv_sem=recv_sem.at[d * shards + j],
            device_id=(s ^ j, c ^ d),
            device_id_type=MESH,
        )

    for j, d in peers:
        transfer(j, d, False).start()
    own = pltpu.make_async_copy(source.at[s, c], target.at[s, c], own_sem)
    own.start()
    own.wait()
    for j, d in peers:
        transfer(j, d, True).wait_recv()
    for j, d in peers:
        transfer(j, d, False).wait_send()


def deliver(block):
    shards, groups = block.shape[:2]
    return pl.pallas_call(
        functools.partial(deliver_kernel, shards, groups),
        out_shape=jax.ShapeDtypeStruct(block.shape, block.dtype),
        in_specs=[WHOLE],
        out_specs=ANY,
        scratch_shapes=[
            pltpu.SemaphoreType.DMA,
            pltpu.SemaphoreType.DMA((shards * groups,)),
            pltpu.SemaphoreType.DMA((shards * groups,)),
        ],
        compiler_params=pltpu.CompilerParams(collective_id=2, has_side_effects=True),
        name="deliver",
    )(block)


def halves(data):
    high = data.astype(jnp.bfloat16)
    return high, (data - high.astype(jnp.float32)).astype(jnp.bfloat16)


def product(matrix, which, high, low):
    def dot(a, b):
        return jnp.dot(a, b, preferred_element_type=jnp.float32)

    return (
        dot(matrix[which], high) + dot(matrix[which], low) + dot(matrix[which + 1], high)
    )


def spectral_kernel(side, coef, held, turn, matrix, filt, other, grad, away, packed, work):
    shards, groups, _, rows, lanes = held.shape
    length = groups * rows
    total = 2 * length * shards
    part = rows * 2 // shards
    step = pl.program_id(0)
    sign = (1 - 2 * side[0]).astype(jnp.float32)

    for g in range(groups):
        here = pl.ds(g * rows, rows)
        for sig in range(2):
            sums = [[None, None], [None, None]]
            for i in range(shards):
                left = held[i, g, 0 if sig == 0 else 3].astype(jnp.float32)
                right = held[i, g, 1 if sig == 0 else 2].astype(jnp.float32)
                value = left * right
                for p in range(2):
                    term = value * coef[step * 2 + p, i]
                    sums[p][i % 2] = term if i < 2 else sums[p][i % 2] + term
            for w in range(2):
                real, imag = (
                    sums[p][0] + sums[p][1] if w == 0 else sums[p][0] - sums[p][1]
                    for p in range(2)
                )
                cos, sin = turn[w, 0, 0, here], turn[w, 0, 1, here]
                at = (w * 2 + sig) * 2 * lanes
                work[here, at : at + lanes] = real * cos + imag * sin
                work[here, at + lanes : at + 2 * lanes] = imag * cos - real * sin
    span = 2 * lanes
    found = []
    for w in range(2):
        spectra = []
        for sig in range(2):
            at = (w * 2 + sig) * span
            high, low = halves(work[:, at : at + span])
            by_cos = product(matrix, 0, high, low)
            by_sin = product(matrix, 2, high, low)
            spectra.append(by_cos[:, :lanes] + by_sin[:, lanes:])
            spectra.append(by_cos[:, lanes:] - by_sin[:, :lanes])
        sr, si, cr, ci = spectra
        spectrum, slope = ((filt, grad), (other, away))[w]
        fr, fi = spectrum[0, 0, 0], spectrum[1, 0, 0]
        slope[0, 0, 0] = (sr * cr + si * ci) * (1.0 / total)
        slope[1, 0, 0] = (sr * ci - si * cr) * (1.0 / total)
        real = (sr * fr - si * fi) - (fr * ci - fi * cr)
        imag = (sr * fi + si * fr) + (fr * cr + fi * ci)
        high, low = halves(jnp.concatenate([real, imag], axis=1))
        by_cos = product(matrix, 0, high, low)
        by_sin = product(matrix, 2, high, low)
        real = by_cos[:, :lanes] - by_sin[:, lanes:]
        imag = by_cos[:, lanes:] + by_sin[:, :lanes]
        cos, sin = turn[w, 0, 0] * (1.0 / total), turn[w, 0, 1] * (1.0 / total)
        found.append((real * cos - imag * sin, real * sin + imag * cos))
    for p in range(2):
        done = (found[0][p] + found[1][p], (found[0][p] - found[1][p]) * sign)
        for v in range(2):
            for k in range(shards // 2):
                for g in range(groups):
                    at = g * rows + k * part
                    packed[k, v, 0, p, g * part : (g + 1) * part] = done[v][at : at + part]


def spectral(side, coef, held, turn, matrix, filt, other):
    shards, groups, _, rows, lanes = held.shape
    length = groups * rows
    pairs = shards // 2
    part = length // pairs
    half_block = pl.BlockSpec((2, 1, 1, length, lanes), lambda n, side: (0, 0, n, 0, 0))
    return pl.pallas_call(
        spectral_kernel,
        grid_spec=pltpu.PrefetchScalarGridSpec(
            num_scalar_prefetch=1,
            grid=(2,),
            in_specs=[
                pl.BlockSpec(memory_space=pltpu.SMEM),
                pl.BlockSpec((shards, groups, 4, rows, lanes), lambda n, side: (0, 0, 0, 0, 0)),
                pl.BlockSpec((2, 1, 2, length, lanes), lambda n, side: (0, n, 0, 0, 0)),
                pl.BlockSpec((4, length, length), lambda n, side: (0, 0, 0)),
                pl.BlockSpec((2, 1, 1, length, lanes), lambda n, side: (0, 0, n, 0, side[0])),
                half_block,
            ],
            out_specs=(
                half_block,
                half_block,
                pl.BlockSpec((pairs, 2, 1, 2, part, lanes), lambda n, side: (0, 0, n, 0, 0, 0)),
            ),
            scratch_shapes=[pltpu.VMEM((length, 8 * lanes), jnp.float32)],
        ),
        out_shape=(
            jax.ShapeDtypeStruct(other.shape, jnp.float32),
            jax.ShapeDtypeStruct(other.shape, jnp.float32),
            jax.ShapeDtypeStruct((pairs, 2, 2, 2, part, lanes), jnp.float32),
        ),
        compiler_params=pltpu.CompilerParams(vmem_limit_bytes=60 * 1024 * 1024),
        name="spectral",
    )(side, coef, held, turn, matrix, filt, other)


def rotate(value, numerator, denominator):
    numerator = numerator % denominator
    real, imag = value
    if numerator == 0:
        return value
    if 4 * numerator == denominator:
        return (-imag, real)
    angle = 2.0 * math.pi * numerator / denominator
    cos, sin = math.cos(angle), math.sin(angle)
    return (real * cos - imag * sin, real * sin + imag * cos)


def butterflies(values):
    count = len(values)
    if count == 1:
        return values
    even, odd = butterflies(values[0::2]), butterflies(values[1::2])
    out = [None] * count
    for k in range(count // 2):
        turned = rotate(odd[k], k, count)
        out[k] = (even[k][0] + turned[0], even[k][1] + turned[1])
        out[k + count // 2] = (even[k][0] - turned[0], even[k][1] - turned[1])
    return out


def finish_kernel(pieces, gates, result):
    shards, _, _, part, lanes = gates.shape
    pairs = shards // 2
    bits = pairs.bit_length() - 1
    ladders = {}
    for e in range(2):
        for v in range(2):
            terms = []
            for q in range(pairs):
                k = mirrored(q, bits)
                terms.append(rotate((pieces[k, v, e, 0], pieces[k, v, e, 1]), q * v, shards))
            ladders[e, v] = butterflies(terms)
    for i in range(shards):
        plain = ladders[0, i % 2][i // 2]
        odd = rotate(ladders[1, i % 2][i // 2], i, 2 * shards)
        conv = plain[0] + odd[0]
        back = plain[1] + odd[1]
        value = gates[i, 0, 0].astype(jnp.float32)
        gate_in = gates[i, 0, 1].astype(jnp.float32)
        gate_out = gates[i, 0, 2].astype(jnp.float32)
        incoming = gates[i, 0, 3].astype(jnp.float32)
        result[i, 0, 0] = (gate_out * conv).astype(jnp.bfloat16)
        result[i, 0, 1] = (back * gate_in).astype(jnp.bfloat16)
        result[i, 0, 2] = (back * value).astype(jnp.bfloat16)
        result[i, 0, 3] = (incoming * conv).astype(jnp.bfloat16)


def finish(pieces, gates):
    shards, groups, _, part, lanes = gates.shape
    gates_block = pl.BlockSpec((shards, 1, 4, part, lanes), lambda n: (0, n, 0, 0, 0))
    return pl.pallas_call(
        finish_kernel,
        grid=(groups,),
        out_shape=jax.ShapeDtypeStruct(gates.shape, jnp.bfloat16),
        in_specs=[
            pl.BlockSpec((shards // 2, 2, 2, 2, part, lanes), lambda n: (0, 0, 0, 0, n, 0)),
            gates_block,
        ],
        out_specs=gates_block,
        name="finish",
    )(pieces, gates)


def transform_matrix(length):
    counter = np.arange(length)
    angle = 2.0 * math.pi * (np.outer(counter, counter) % length) / length
    out = []
    for table in (np.cos(angle), np.sin(angle)):
        high = table.astype(jnp.bfloat16)
        out += [high, (table - high.astype(np.float64)).astype(jnp.bfloat16)]
    return jnp.asarray(np.stack(out))


def on_device(shards, groups, values_in, gate_in, gate_out, cotangent, filter_spectra):
    rows = values_in.shape[0]
    length = rows * groups
    total = 2 * length * shards
    index = lax.axis_index("seq")
    side = index % 2
    own = 2 * mirrored(index, shards.bit_length() - 1) + jnp.arange(2, dtype=jnp.int32)
    shard = jnp.arange(shards, dtype=jnp.int32)
    angle = (2.0 * math.pi / (2 * shards)) * (own[:, None] * shard[None, :] % (2 * shards)).astype(
        jnp.float32
    )
    coef = jnp.stack([jnp.cos(angle), -jnp.sin(angle)], axis=1).reshape(4, shards)
    position = jnp.arange(length, dtype=jnp.int32)
    residue = jnp.stack([own, (own + shards) % (2 * shards)])
    angle = (2.0 * math.pi / total) * (residue[..., None] * position % total).astype(jnp.float32)
    turn = jnp.stack([jnp.cos(angle), jnp.sin(angle)], axis=2)
    turn = jnp.broadcast_to(turn[..., None], (2, 2, 2, length, 128))

    held, other = gather(
        (values_in, gate_in, gate_out, cotangent), filter_spectra, shards, groups
    )
    mine, away, packed = spectral(
        side[None], coef, held, turn, transform_matrix(length), filter_spectra, other
    )
    pieces, theirs = trade(packed, away)
    part = rows * 2 // shards
    gates = lax.dynamic_slice_in_dim(held, index // 2 * part, part, axis=3)
    result = deliver(finish(pieces, gates))
    result = result.reshape((shards // 2, 2) + result.shape[1:])
    outs = [
        result[:, :, :, a].transpose(0, 3, 2, 1, 4).reshape(rows, values_in.shape[1])
        for a in range(4)
    ]
    grad_filter = jnp.concatenate(
        [jnp.where(side == 0, mine, theirs), jnp.where(side == 0, theirs, mine)], axis=-1
    )
    return (outs[0], outs[1], outs[2], outs[3], grad_filter)


def solution(mesh):
    tokens = P(("seq", "chan"), None)
    spectrum = P(None, "seq", None, None, "chan")
    return jax.shard_map(
        functools.partial(on_device, mesh.shape["seq"], mesh.shape["chan"]),
        mesh=mesh,
        in_specs=(tokens, tokens, tokens, tokens, spectrum),
        out_specs=(tokens, tokens, tokens, tokens, spectrum),
        check_vma=False,
    )
```

```python
import functools
import math

import jax
import jax.numpy as jnp
import numpy as np
from jax import lax
from jax.experimental import pallas as pl
from jax.experimental.pallas import tpu as pltpu
from jax.sharding import PartitionSpec as P

MESH = pl.DeviceIdType.MESH
ANY = pl.BlockSpec(memory_space=pl.ANY)
WHOLE = pl.BlockSpec(memory_space=pltpu.VMEM)


def mirrored(number, bits):
    out = 0
    for place in range(bits):
        out = out + ((number >> place) & 1) * (1 << (bits - 1 - place))
    return out


def meet(peers):
    barrier = pltpu.get_barrier_semaphore()
    for peer in peers:
        pl.semaphore_signal(barrier, inc=1, device_id=peer, device_id_type=MESH)
    pl.semaphore_wait(barrier, len(peers))


def gather_kernel(shards, groups, *refs):
    source, filt, held, other = refs[:4]
    own_sem, z_send, z_recv, s_send, s_recv, f_send, f_recv = refs[4:]
    s, c = lax.axis_index("seq"), lax.axis_index("chan")
    half = s % 2
    pair = s // 2
    lanes = source.shape[-1]
    bits = shards.bit_length() - 1
    near = [(d, e) for d in range(groups) for e in range(2) if d or e]
    meet([(s ^ e, c ^ d) for d, e in near] + [(s ^ (1 << b), c) for b in range(1, bits)])

    def cross(d, e, landing):
        return pltpu.make_async_remote_copy(
            src_ref=source.at[c ^ d, half ^ e],
            dst_ref=held.at[s ^ e, c ^ d] if landing else held.at[s, c],
            send_sem=z_send.at[d * 2 + e],
            recv_sem=z_recv.at[d * 2 + e],
            device_id=(s ^ e, c ^ d),
            device_id_type=MESH,
        )

    for d, e in near:
        cross(d, e, False).start()
    own = pltpu.make_async_copy(source.at[c, half], held.at[s, c], own_sem)
    own.start()
    swap = pltpu.make_async_remote_copy(
        src_ref=filt.at[:, :, :, :, pl.ds(pl.multiple_of((half ^ 1) * lanes, lanes), lanes)],
        dst_ref=other,
        send_sem=f_send,
        recv_sem=f_recv,
        device_id=(s ^ 1, c),
        device_id_type=MESH,
    )

    def piece(d, owner, slot, partner):
        place = held.at[pl.ds(owner * 2, 2), c ^ d]
        return pltpu.make_async_remote_copy(
            src_ref=place,
            dst_ref=place,
            send_sem=s_send.at[d * (shards // 2) + slot],
            recv_sem=s_recv.at[d * (shards // 2) + slot],
            device_id=(partner * 2 + half, c),
            device_id_type=MESH,
        )

    far = list(range(bits - 1))
    sent, landed = [], []
    for tick in range(groups + bits):
        for d in range(groups):
            order = far if d % 2 == 0 else far[::-1]
            depth = tick - d
            for mask in range(shards // 2):
                if bin(mask).count("1") != depth:
                    continue
                last = max([order.index(b) for b in far if mask >> b & 1], default=-1)
                later = order[last + 1 :]
                if not later:
                    landed.append((d, mask))
                    continue
                if mask:
                    piece(d, pair ^ mask, mask, pair).wait_recv()
                else:
                    for e in range(2):
                        if d or e:
                            cross(d, e, True).wait_recv()
                        else:
                            own.wait()
                for b in later:
                    copy = piece(d, pair ^ mask, mask ^ (1 << b), pair ^ (1 << b))
                    copy.start()
                    sent.append(copy)
        if tick == 0:
            swap.start()
    for d, mask in landed:
        piece(d, pair ^ mask, mask, pair).wait_recv()
    swap.wait_recv()
    for d, e in near:
        cross(d, e, False).wait_send()
    for copy in sent:
        copy.wait_send()
    swap.wait_send()


def arrange_kernel(*refs):
    lanes = refs[4].shape[-1]
    for side in range(2):
        for a in range(4):
            refs[4][0, side, a] = refs[a][:, side * lanes : (side + 1) * lanes]


def arrange(inputs, groups):
    rows, channels = inputs[0].shape
    width = channels // groups
    lanes = width // 2
    return pl.pallas_call(
        arrange_kernel,
        grid=(groups,),
        out_shape=jax.ShapeDtypeStruct((groups, 2, 4, rows, lanes), inputs[0].dtype),
        in_specs=[pl.BlockSpec((rows, width), lambda n: (0, n))] * 4,
        out_specs=pl.BlockSpec((1, 2, 4, rows, lanes), lambda n: (n, 0, 0, 0, 0)),
        name="arrange",
    )(*inputs)


def gather(source, filt, shards):
    groups, _, _, rows, lanes = source.shape
    return pl.pallas_call(
        functools.partial(gather_kernel, shards, groups),
        out_shape=(
            jax.ShapeDtypeStruct((shards, groups, 4, rows, lanes), source.dtype),
            jax.ShapeDtypeStruct(filt.shape[:-1] + (lanes,), filt.dtype),
        ),
        in_specs=[WHOLE, ANY],
        out_specs=(ANY, ANY),
        scratch_shapes=[
            pltpu.SemaphoreType.DMA,
            pltpu.SemaphoreType.DMA((groups * 2,)),
            pltpu.SemaphoreType.DMA((groups * 2,)),
            pltpu.SemaphoreType.DMA((groups * shards // 2,)),
            pltpu.SemaphoreType.DMA((groups * shards // 2,)),
            pltpu.SemaphoreType.DMA,
            pltpu.SemaphoreType.DMA,
        ],
        compiler_params=pltpu.CompilerParams(collective_id=0, has_side_effects=True),
        name="gather",
    )(source, filt)


def trade_kernel(shards, source, grad, target, other, own_sem, send_sem, recv_sem):
    s, c = lax.axis_index("seq"), lax.axis_index("chan")
    pairs = shards // 2
    pair, half = s // 2, s % 2
    meet([((pair ^ j) * 2 + half, c) for j in range(1, pairs)] + [(s ^ 1, c)])

    def transfer(j, landing):
        return pltpu.make_async_remote_copy(
            src_ref=source.at[pair ^ j],
            dst_ref=target.at[pair ^ j] if landing else target.at[pair],
            send_sem=send_sem.at[j],
            recv_sem=recv_sem.at[j],
            device_id=((pair ^ j) * 2 + half, c),
            device_id_type=MESH,
        )

    swap = pltpu.make_async_remote_copy(
        src_ref=grad,
        dst_ref=other,
        send_sem=send_sem.at[0],
        recv_sem=recv_sem.at[0],
        device_id=(s ^ 1, c),
        device_id_type=MESH,
    )
    for j in range(pairs - 1, 0, -1):
        transfer(j, False).start()
    swap.start()
    own = pltpu.make_async_copy(source.at[pair], target.at[pair], own_sem)
    own.start()
    own.wait()
    swap.wait_recv()
    for j in range(1, pairs):
        transfer(j, True).wait_recv()
    for j in range(1, pairs):
        transfer(j, False).wait_send()
    swap.wait_send()


def trade(block, grad):
    pairs = block.shape[0]
    return pl.pallas_call(
        functools.partial(trade_kernel, 2 * pairs),
        out_shape=(
            jax.ShapeDtypeStruct(block.shape, block.dtype),
            jax.ShapeDtypeStruct(grad.shape, grad.dtype),
        ),
        in_specs=[WHOLE, ANY],
        out_specs=(ANY, ANY),
        scratch_shapes=[
            pltpu.SemaphoreType.DMA,
            pltpu.SemaphoreType.DMA((pairs,)),
            pltpu.SemaphoreType.DMA((pairs,)),
        ],
        compiler_params=pltpu.CompilerParams(collective_id=1, has_side_effects=True),
        name="trade",
    )(block, grad)


def deliver_kernel(shards, groups, source, target, own_sem, send_sem, recv_sem):
    s, c = lax.axis_index("seq"), lax.axis_index("chan")
    peers = [(j, d) for d in range(groups - 1, -1, -1) for j in range(shards) if j or d]
    meet([(s ^ j, c ^ d) for j, d in peers])

    part, lanes = source.shape[-2:]

    def place(shard, group):
        rows = pl.ds(pl.multiple_of(shard // 2 * part, part), part)
        return target.at[
            :, rows, pl.ds(pl.multiple_of((group * 2 + shard % 2) * lanes, lanes), lanes)
        ]

    def transfer(j, d, landing):
        to_s, to_c = (s ^ j, c ^ d) if landing else (s, c)
        return pltpu.make_async_remote_copy(
            src_ref=source.at[s ^ j, c ^ d],
            dst_ref=place(to_s, to_c),
            send_sem=send_sem.at[d * shards + j],
            recv_sem=recv_sem.at[d * shards + j],
            device_id=(s ^ j, c ^ d),
            device_id_type=MESH,
        )

    for j, d in peers:
        transfer(j, d, False).start()
    own = pltpu.make_async_copy(source.at[s, c], place(s, c), own_sem)
    own.start()
    own.wait()
    for j, d in peers:
        transfer(j, d, True).wait_recv()
    for j, d in peers:
        transfer(j, d, False).wait_send()


def deliver(block):
    shards, groups, _, part, lanes = block.shape
    return pl.pallas_call(
        functools.partial(deliver_kernel, shards, groups),
        out_shape=jax.ShapeDtypeStruct(
            (4, part * shards // 2, groups * 2 * lanes), block.dtype
        ),
        in_specs=[WHOLE],
        out_specs=ANY,
        scratch_shapes=[
            pltpu.SemaphoreType.DMA,
            pltpu.SemaphoreType.DMA((shards * groups,)),
            pltpu.SemaphoreType.DMA((shards * groups,)),
        ],
        compiler_params=pltpu.CompilerParams(collective_id=2, has_side_effects=True),
        name="deliver",
    )(block)


def halves(data):
    high = data.astype(jnp.bfloat16)
    return high, (data - high.astype(jnp.float32)).astype(jnp.bfloat16)


def product(matrix, which, high, low):
    def dot(a, b):
        return jnp.dot(a, b, preferred_element_type=jnp.float32)

    return (
        dot(matrix[which], high) + dot(matrix[which], low) + dot(matrix[which + 1], high)
    )


def spectral_kernel(side, coef, held, turn, matrix, filt, other, grad, away, packed, work):
    shards, groups, _, rows, lanes = held.shape
    length = groups * rows
    total = 2 * length * shards
    part = rows * 2 // shards
    step = pl.program_id(0)
    sign = (1 - 2 * side[0]).astype(jnp.float32)
    turns = jnp.transpose(turn[0])

    def twiddle(w, here):
        return (turns[here, 2 * w : 2 * w + 1], turns[here, 2 * w + 1 : 2 * w + 2])

    for g in range(groups):
        here = pl.ds(g * rows, rows)
        for sig in range(2):
            sums = [[None, None], [None, None]]
            for i in range(shards):
                left = held[i, g, 0 if sig == 0 else 3].astype(jnp.float32)
                right = held[i, g, 1 if sig == 0 else 2].astype(jnp.float32)
                value = left * right
                for p in range(2):
                    term = value * coef[step * 2 + p, i]
                    sums[p][i % 2] = term if i < 2 else sums[p][i % 2] + term
            for w in range(2):
                real, imag = (
                    sums[p][0] + sums[p][1] if w == 0 else sums[p][0] - sums[p][1]
                    for p in range(2)
                )
                cos, sin = twiddle(w, slice(g * rows, (g + 1) * rows))
                at = (w * 2 + sig) * 2 * lanes
                work[here, at : at + lanes] = real * cos + imag * sin
                work[here, at + lanes : at + 2 * lanes] = imag * cos - real * sin
    span = 2 * lanes
    found = []
    for w in range(2):
        spectra = []
        for sig in range(2):
            at = (w * 2 + sig) * span
            high, low = halves(work[:, at : at + span])
            by_cos = product(matrix, 0, high, low)
            by_sin = product(matrix, 2, high, low)
            spectra.append(by_cos[:, :lanes] + by_sin[:, lanes:])
            spectra.append(by_cos[:, lanes:] - by_sin[:, :lanes])
        sr, si, cr, ci = spectra
        spectrum, slope = ((filt, grad), (other, away))[w]
        fr, fi = spectrum[0, 0, 0], spectrum[1, 0, 0]
        slope[0, 0, 0] = (sr * cr + si * ci) * (1.0 / total)
        slope[1, 0, 0] = (sr * ci - si * cr) * (1.0 / total)
        real = (sr * fr - si * fi) - (fr * ci - fi * cr)
        imag = (sr * fi + si * fr) + (fr * cr + fi * ci)
        high, low = halves(jnp.concatenate([real, imag], axis=1))
        by_cos = product(matrix, 0, high, low)
        by_sin = product(matrix, 2, high, low)
        real = by_cos[:, :lanes] - by_sin[:, lanes:]
        imag = by_cos[:, lanes:] + by_sin[:, :lanes]
        cos, sin = (table * (1.0 / total) for table in twiddle(w, slice(None)))
        found.append((real * cos - imag * sin, real * sin + imag * cos))
    for p in range(2):
        done = (found[0][p] + found[1][p], (found[0][p] - found[1][p]) * sign)
        for v in range(2):
            for k in range(shards // 2):
                for g in range(groups):
                    at = g * rows + k * part
                    packed[k, v, 0, p, g * part : (g + 1) * part] = done[v][at : at + part]


def spectral(side, coef, held, turn, matrix, filt, other):
    shards, groups, _, rows, lanes = held.shape
    length = groups * rows
    pairs = shards // 2
    part = length // pairs
    half_block = pl.BlockSpec((2, 1, 1, length, lanes), lambda n, side: (0, 0, n, 0, 0))
    return pl.pallas_call(
        spectral_kernel,
        grid_spec=pltpu.PrefetchScalarGridSpec(
            num_scalar_prefetch=1,
            grid=(2,),
            in_specs=[
                pl.BlockSpec(memory_space=pltpu.SMEM),
                pl.BlockSpec((shards, groups, 4, rows, lanes), lambda n, side: (0, 0, 0, 0, 0)),
                pl.BlockSpec((1, 8, length), lambda n, side: (n, 0, 0)),
                pl.BlockSpec((4, length, length), lambda n, side: (0, 0, 0)),
                pl.BlockSpec((2, 1, 1, length, lanes), lambda n, side: (0, 0, n, 0, side[0])),
                half_block,
            ],
            out_specs=(
                half_block,
                half_block,
                pl.BlockSpec((pairs, 2, 1, 2, part, lanes), lambda n, side: (0, 0, n, 0, 0, 0)),
            ),
            scratch_shapes=[pltpu.VMEM((length, 8 * lanes), jnp.float32)],
        ),
        out_shape=(
            jax.ShapeDtypeStruct(other.shape, jnp.float32),
            jax.ShapeDtypeStruct(other.shape, jnp.float32),
            jax.ShapeDtypeStruct((pairs, 2, 2, 2, part, lanes), jnp.float32),
        ),
        compiler_params=pltpu.CompilerParams(vmem_limit_bytes=60 * 1024 * 1024),
        name="spectral",
    )(side, coef, held, turn, matrix, filt, other)


def rotate(value, numerator, denominator):
    numerator = numerator % denominator
    real, imag = value
    if numerator == 0:
        return value
    if 4 * numerator == denominator:
        return (-imag, real)
    angle = 2.0 * math.pi * numerator / denominator
    cos, sin = math.cos(angle), math.sin(angle)
    return (real * cos - imag * sin, real * sin + imag * cos)


def butterflies(values):
    count = len(values)
    if count == 1:
        return values
    even, odd = butterflies(values[0::2]), butterflies(values[1::2])
    out = [None] * count
    for k in range(count // 2):
        turned = rotate(odd[k], k, count)
        out[k] = (even[k][0] + turned[0], even[k][1] + turned[1])
        out[k + count // 2] = (even[k][0] - turned[0], even[k][1] - turned[1])
    return out


def finish_kernel(pair, pieces, gates, result):
    shards, _, _, part, lanes = gates.shape
    pairs = shards // 2
    bits = pairs.bit_length() - 1
    ladders = {}
    for e in range(2):
        for v in range(2):
            terms = []
            for q in range(pairs):
                k = mirrored(q, bits)
                terms.append(rotate((pieces[k, v, e, 0], pieces[k, v, e, 1]), q * v, shards))
            ladders[e, v] = butterflies(terms)
    for i in range(shards):
        plain = ladders[0, i % 2][i // 2]
        odd = rotate(ladders[1, i % 2][i // 2], i, 2 * shards)
        conv = plain[0] + odd[0]
        back = plain[1] + odd[1]
        value = gates[i, 0, 0].astype(jnp.float32)
        gate_in = gates[i, 0, 1].astype(jnp.float32)
        gate_out = gates[i, 0, 2].astype(jnp.float32)
        incoming = gates[i, 0, 3].astype(jnp.float32)
        result[i, 0, 0] = (gate_out * conv).astype(jnp.bfloat16)
        result[i, 0, 1] = (back * gate_in).astype(jnp.bfloat16)
        result[i, 0, 2] = (back * value).astype(jnp.bfloat16)
        result[i, 0, 3] = (incoming * conv).astype(jnp.bfloat16)


def finish(pair, pieces, held):
    shards, groups, _, rows, lanes = held.shape
    part = rows * 2 // shards
    block = (shards, 1, 4, part, lanes)
    return pl.pallas_call(
        finish_kernel,
        grid_spec=pltpu.PrefetchScalarGridSpec(
            num_scalar_prefetch=1,
            grid=(groups,),
            in_specs=[
                pl.BlockSpec((shards // 2, 2, 2, 2, part, lanes), lambda n, k: (0, 0, 0, 0, n, 0)),
                pl.BlockSpec(block, lambda n, k: (0, n, 0, k[0], 0)),
            ],
            out_specs=pl.BlockSpec(block, lambda n, k: (0, n, 0, 0, 0)),
        ),
        out_shape=jax.ShapeDtypeStruct((shards, groups, 4, part, lanes), jnp.bfloat16),
        name="finish",
    )(pair[None], pieces, held)


def transform_matrix(length):
    counter = np.arange(length)
    angle = 2.0 * math.pi * (np.outer(counter, counter) % length) / length
    out = []
    for table in (np.cos(angle), np.sin(angle)):
        high = table.astype(jnp.bfloat16)
        out += [high, (table - high.astype(np.float64)).astype(jnp.bfloat16)]
    return jnp.asarray(np.stack(out))


def on_device(shards, groups, values_in, gate_in, gate_out, cotangent, filter_spectra):
    rows = values_in.shape[0]
    length = rows * groups
    total = 2 * length * shards
    index = lax.axis_index("seq")
    side = index % 2
    own = 2 * mirrored(index, shards.bit_length() - 1) + jnp.arange(2, dtype=jnp.int32)
    shard = jnp.arange(shards, dtype=jnp.int32)
    angle = (2.0 * math.pi / (2 * shards)) * (own[:, None] * shard[None, :] % (2 * shards)).astype(
        jnp.float32
    )
    coef = jnp.stack([jnp.cos(angle), -jnp.sin(angle)], axis=1).reshape(4, shards)
    position = jnp.arange(length, dtype=jnp.int32)
    residue = jnp.stack([own, (own + shards) % (2 * shards)], axis=1)
    angle = (2.0 * math.pi / total) * (residue[..., None] * position % total).astype(jnp.float32)
    turn = jnp.stack([jnp.cos(angle), jnp.sin(angle)], axis=2).reshape(2, 4, length)
    turn = jnp.concatenate([turn, jnp.zeros_like(turn)], axis=1)

    source = arrange((values_in, gate_in, gate_out, cotangent), groups)
    held, other = gather(source, filter_spectra, shards)
    mine, away, packed = spectral(
        side[None], coef, held, turn, transform_matrix(length), filter_spectra, other
    )
    pieces, theirs = trade(packed, away)
    outs = deliver(finish(index // 2, pieces, held))
    grad_filter = jnp.concatenate(
        [jnp.where(side == 0, mine, theirs), jnp.where(side == 0, theirs, mine)], axis=-1
    )
    return (outs[0], outs[1], outs[2], outs[3], grad_filter)


def solution(mesh):
    tokens = P(("seq", "chan"), None)
    spectrum = P(None, "seq", None, None, "chan")
    return jax.shard_map(
        functools.partial(on_device, mesh.shape["seq"], mesh.shape["chan"]),
        mesh=mesh,
        in_specs=(tokens, tokens, tokens, tokens, spectrum),
        out_specs=(tokens, tokens, tokens, tokens, spectrum),
        check_vma=False,
    )
```

```python
import functools
import math

import jax
import jax.numpy as jnp
import numpy as np
from jax import lax
from jax.experimental import pallas as pl
from jax.experimental.pallas import tpu as pltpu
from jax.sharding import PartitionSpec as P

MESH = pl.DeviceIdType.MESH
ANY = pl.BlockSpec(memory_space=pl.ANY)
WHOLE = pl.BlockSpec(memory_space=pltpu.VMEM)


def mirrored(number, bits):
    out = 0
    for place in range(bits):
        out = out + ((number >> place) & 1) * (1 << (bits - 1 - place))
    return out


def meet(peers):
    barrier = pltpu.get_barrier_semaphore()
    for peer in peers:
        pl.semaphore_signal(barrier, inc=1, device_id=peer, device_id_type=MESH)
    pl.semaphore_wait(barrier, len(peers))


def gather_kernel(shards, groups, *refs):
    source, filt, held, other = refs[:4]
    own_sem, z_send, z_recv, s_send, s_recv, f_send, f_recv = refs[4:]
    s, c = lax.axis_index("seq"), lax.axis_index("chan")
    half = s % 2
    pair = s // 2
    lanes = source.shape[-1]
    bits = shards.bit_length() - 1
    near = [(d, e) for d in range(groups) for e in range(2) if d or e]
    meet([(s ^ e, c ^ d) for d, e in near] + [(s ^ (1 << b), c) for b in range(1, bits)])

    def cross(d, e, landing):
        return pltpu.make_async_remote_copy(
            src_ref=source.at[c ^ d, half ^ e],
            dst_ref=held.at[s ^ e, c ^ d] if landing else held.at[s, c],
            send_sem=z_send.at[d * 2 + e],
            recv_sem=z_recv.at[d * 2 + e],
            device_id=(s ^ e, c ^ d),
            device_id_type=MESH,
        )

    for d, e in near:
        cross(d, e, False).start()
    own = pltpu.make_async_copy(source.at[c, half], held.at[s, c], own_sem)
    own.start()
    swap = pltpu.make_async_remote_copy(
        src_ref=filt.at[:, :, :, :, pl.ds(pl.multiple_of((half ^ 1) * lanes, lanes), lanes)],
        dst_ref=other,
        send_sem=f_send,
        recv_sem=f_recv,
        device_id=(s ^ 1, c),
        device_id_type=MESH,
    )

    def piece(d, owner, slot, partner):
        place = held.at[pl.ds(owner * 2, 2), c ^ d]
        return pltpu.make_async_remote_copy(
            src_ref=place,
            dst_ref=place,
            send_sem=s_send.at[d * (shards // 2) + slot],
            recv_sem=s_recv.at[d * (shards // 2) + slot],
            device_id=(partner * 2 + half, c),
            device_id_type=MESH,
        )

    far = list(range(bits - 1))
    sent, landed = [], []
    for tick in range((groups + 1) // 2 * bits):
        for d in range(groups):
            order = far if d % 2 == 0 else far[::-1]
            depth = tick - d // 2 * bits
            for mask in range(shards // 2):
                if bin(mask).count("1") != depth:
                    continue
                last = max([order.index(b) for b in far if mask >> b & 1], default=-1)
                later = order[last + 1 :]
                if not later:
                    landed.append((d, mask))
                    continue
                if mask:
                    piece(d, pair ^ mask, mask, pair).wait_recv()
                else:
                    for e in range(2):
                        if d or e:
                            cross(d, e, True).wait_recv()
                        else:
                            own.wait()
                for b in later:
                    copy = piece(d, pair ^ mask, mask ^ (1 << b), pair ^ (1 << b))
                    copy.start()
                    sent.append(copy)
        if tick == 0:
            swap.start()
    for d, mask in landed:
        piece(d, pair ^ mask, mask, pair).wait_recv()
    swap.wait_recv()
    for d, e in near:
        cross(d, e, False).wait_send()
    for copy in sent:
        copy.wait_send()
    swap.wait_send()


def arrange_kernel(*refs):
    lanes = refs[4].shape[-1]
    for side in range(2):
        for a in range(4):
            refs[4][0, side, a] = refs[a][:, side * lanes : (side + 1) * lanes]


def arrange(inputs, groups):
    rows, channels = inputs[0].shape
    width = channels // groups
    lanes = width // 2
    return pl.pallas_call(
        arrange_kernel,
        grid=(groups,),
        out_shape=jax.ShapeDtypeStruct((groups, 2, 4, rows, lanes), inputs[0].dtype),
        in_specs=[pl.BlockSpec((rows, width), lambda n: (0, n))] * 4,
        out_specs=pl.BlockSpec((1, 2, 4, rows, lanes), lambda n: (n, 0, 0, 0, 0)),
        name="arrange",
    )(*inputs)


def gather(source, filt, shards):
    groups, _, _, rows, lanes = source.shape
    return pl.pallas_call(
        functools.partial(gather_kernel, shards, groups),
        out_shape=(
            jax.ShapeDtypeStruct((shards, groups, 4, rows, lanes), source.dtype),
            jax.ShapeDtypeStruct(filt.shape[:-1] + (lanes,), filt.dtype),
        ),
        in_specs=[WHOLE, ANY],
        out_specs=(ANY, ANY),
        scratch_shapes=[
            pltpu.SemaphoreType.DMA,
            pltpu.SemaphoreType.DMA((groups * 2,)),
            pltpu.SemaphoreType.DMA((groups * 2,)),
            pltpu.SemaphoreType.DMA((groups * shards // 2,)),
            pltpu.SemaphoreType.DMA((groups * shards // 2,)),
            pltpu.SemaphoreType.DMA,
            pltpu.SemaphoreType.DMA,
        ],
        compiler_params=pltpu.CompilerParams(collective_id=0, has_side_effects=True),
        name="gather",
    )(source, filt)


def trade_kernel(shards, source, grad, target, other, own_sem, send_sem, recv_sem):
    s, c = lax.axis_index("seq"), lax.axis_index("chan")
    pairs = shards // 2
    pair, half = s // 2, s % 2
    meet([((pair ^ j) * 2 + half, c) for j in range(1, pairs)] + [(s ^ 1, c)])

    def transfer(j, landing):
        return pltpu.make_async_remote_copy(
            src_ref=source.at[pair ^ j],
            dst_ref=target.at[pair ^ j] if landing else target.at[pair],
            send_sem=send_sem.at[j],
            recv_sem=recv_sem.at[j],
            device_id=((pair ^ j) * 2 + half, c),
            device_id_type=MESH,
        )

    swap = pltpu.make_async_remote_copy(
        src_ref=grad,
        dst_ref=other,
        send_sem=send_sem.at[0],
        recv_sem=recv_sem.at[0],
        device_id=(s ^ 1, c),
        device_id_type=MESH,
    )
    for j in range(pairs - 1, 0, -1):
        transfer(j, False).start()
    swap.start()
    own = pltpu.make_async_copy(source.at[pair], target.at[pair], own_sem)
    own.start()
    own.wait()
    swap.wait_recv()
    for j in range(1, pairs):
        transfer(j, True).wait_recv()
    for j in range(1, pairs):
        transfer(j, False).wait_send()
    swap.wait_send()


def trade(block, grad):
    pairs = block.shape[0]
    return pl.pallas_call(
        functools.partial(trade_kernel, 2 * pairs),
        out_shape=(
            jax.ShapeDtypeStruct(block.shape, block.dtype),
            jax.ShapeDtypeStruct(grad.shape, grad.dtype),
        ),
        in_specs=[WHOLE, ANY],
        out_specs=(ANY, ANY),
        scratch_shapes=[
            pltpu.SemaphoreType.DMA,
            pltpu.SemaphoreType.DMA((pairs,)),
            pltpu.SemaphoreType.DMA((pairs,)),
        ],
        compiler_params=pltpu.CompilerParams(collective_id=1, has_side_effects=True),
        name="trade",
    )(block, grad)


def deliver_kernel(shards, groups, source, target, own_sem, send_sem, recv_sem):
    s, c = lax.axis_index("seq"), lax.axis_index("chan")
    peers = [(j, d) for d in range(groups - 1, -1, -1) for j in range(shards) if j or d]
    meet([(s ^ j, c ^ d) for j, d in peers])

    part, lanes = source.shape[-2:]

    def place(shard, group):
        rows = pl.ds(pl.multiple_of(shard // 2 * part, part), part)
        return target.at[
            :, rows, pl.ds(pl.multiple_of((group * 2 + shard % 2) * lanes, lanes), lanes)
        ]

    def transfer(j, d, landing):
        to_s, to_c = (s ^ j, c ^ d) if landing else (s, c)
        return pltpu.make_async_remote_copy(
            src_ref=source.at[s ^ j, c ^ d],
            dst_ref=place(to_s, to_c),
            send_sem=send_sem.at[d * shards + j],
            recv_sem=recv_sem.at[d * shards + j],
            device_id=(s ^ j, c ^ d),
            device_id_type=MESH,
        )

    for j, d in peers:
        transfer(j, d, False).start()
    own = pltpu.make_async_copy(source.at[s, c], place(s, c), own_sem)
    own.start()
    own.wait()
    for j, d in peers:
        transfer(j, d, True).wait_recv()
    for j, d in peers:
        transfer(j, d, False).wait_send()


def deliver(block):
    shards, groups, _, part, lanes = block.shape
    return pl.pallas_call(
        functools.partial(deliver_kernel, shards, groups),
        out_shape=jax.ShapeDtypeStruct(
            (4, part * shards // 2, groups * 2 * lanes), block.dtype
        ),
        in_specs=[WHOLE],
        out_specs=ANY,
        scratch_shapes=[
            pltpu.SemaphoreType.DMA,
            pltpu.SemaphoreType.DMA((shards * groups,)),
            pltpu.SemaphoreType.DMA((shards * groups,)),
        ],
        compiler_params=pltpu.CompilerParams(collective_id=2, has_side_effects=True),
        name="deliver",
    )(block)


def halves(data):
    high = data.astype(jnp.bfloat16)
    return high, (data - high.astype(jnp.float32)).astype(jnp.bfloat16)


def product(matrix, which, high, low):
    def dot(a, b):
        return jnp.dot(a, b, preferred_element_type=jnp.float32)

    return (
        dot(matrix[which], high) + dot(matrix[which], low) + dot(matrix[which + 1], high)
    )


def spectral_kernel(side, coef, held, turn, matrix, filt, other, grad, away, packed, work):
    shards, groups, _, rows, lanes = held.shape
    length = groups * rows
    total = 2 * length * shards
    part = rows * 2 // shards
    step = pl.program_id(0)
    sign = (1 - 2 * side[0]).astype(jnp.float32)
    turns = jnp.transpose(turn[0])

    def twiddle(w, here):
        return (turns[here, 2 * w : 2 * w + 1], turns[here, 2 * w + 1 : 2 * w + 2])

    for g in range(groups):
        here = pl.ds(g * rows, rows)
        for sig in range(2):
            sums = [[None, None], [None, None]]
            for i in range(shards):
                left = held[i, g, 0 if sig == 0 else 3].astype(jnp.float32)
                right = held[i, g, 1 if sig == 0 else 2].astype(jnp.float32)
                value = left * right
                for p in range(2):
                    term = value * coef[step * 2 + p, i]
                    sums[p][i % 2] = term if i < 2 else sums[p][i % 2] + term
            for w in range(2):
                real, imag = (
                    sums[p][0] + sums[p][1] if w == 0 else sums[p][0] - sums[p][1]
                    for p in range(2)
                )
                cos, sin = twiddle(w, slice(g * rows, (g + 1) * rows))
                at = (w * 2 + sig) * 2 * lanes
                work[here, at : at + lanes] = real * cos + imag * sin
                work[here, at + lanes : at + 2 * lanes] = imag * cos - real * sin
    span = 2 * lanes
    found = []
    for w in range(2):
        spectra = []
        for sig in range(2):
            at = (w * 2 + sig) * span
            high, low = halves(work[:, at : at + span])
            by_cos = product(matrix, 0, high, low)
            by_sin = product(matrix, 2, high, low)
            spectra.append(by_cos[:, :lanes] + by_sin[:, lanes:])
            spectra.append(by_cos[:, lanes:] - by_sin[:, :lanes])
        sr, si, cr, ci = spectra
        spectrum, slope = ((filt, grad), (other, away))[w]
        fr, fi = spectrum[0, 0, 0], spectrum[1, 0, 0]
        slope[0, 0, 0] = (sr * cr + si * ci) * (1.0 / total)
        slope[1, 0, 0] = (sr * ci - si * cr) * (1.0 / total)
        real = (sr * fr - si * fi) - (fr * ci - fi * cr)
        imag = (sr * fi + si * fr) + (fr * cr + fi * ci)
        high, low = halves(jnp.concatenate([real, imag], axis=1))
        by_cos = product(matrix, 0, high, low)
        by_sin = product(matrix, 2, high, low)
        real = by_cos[:, :lanes] - by_sin[:, lanes:]
        imag = by_cos[:, lanes:] + by_sin[:, :lanes]
        cos, sin = (table * (1.0 / total) for table in twiddle(w, slice(None)))
        found.append((real * cos - imag * sin, real * sin + imag * cos))
    for p in range(2):
        done = (found[0][p] + found[1][p], (found[0][p] - found[1][p]) * sign)
        for v in range(2):
            for k in range(shards // 2):
                for g in range(groups):
                    at = g * rows + k * part
                    packed[k, v, 0, p, g * part : (g + 1) * part] = done[v][at : at + part]


def spectral(side, coef, held, turn, matrix, filt, other):
    shards, groups, _, rows, lanes = held.shape
    length = groups * rows
    pairs = shards // 2
    part = length // pairs
    half_block = pl.BlockSpec((2, 1, 1, length, lanes), lambda n, side: (0, 0, n, 0, 0))
    return pl.pallas_call(
        spectral_kernel,
        grid_spec=pltpu.PrefetchScalarGridSpec(
            num_scalar_prefetch=1,
            grid=(2,),
            in_specs=[
                pl.BlockSpec(memory_space=pltpu.SMEM),
                pl.BlockSpec((shards, groups, 4, rows, lanes), lambda n, side: (0, 0, 0, 0, 0)),
                pl.BlockSpec((1, 8, length), lambda n, side: (n, 0, 0)),
                pl.BlockSpec((4, length, length), lambda n, side: (0, 0, 0)),
                pl.BlockSpec((2, 1, 1, length, lanes), lambda n, side: (0, 0, n, 0, side[0])),
                half_block,
            ],
            out_specs=(
                half_block,
                half_block,
                pl.BlockSpec((pairs, 2, 1, 2, part, lanes), lambda n, side: (0, 0, n, 0, 0, 0)),
            ),
            scratch_shapes=[pltpu.VMEM((length, 8 * lanes), jnp.float32)],
        ),
        out_shape=(
            jax.ShapeDtypeStruct(other.shape, jnp.float32),
            jax.ShapeDtypeStruct(other.shape, jnp.float32),
            jax.ShapeDtypeStruct((pairs, 2, 2, 2, part, lanes), jnp.float32),
        ),
        compiler_params=pltpu.CompilerParams(vmem_limit_bytes=60 * 1024 * 1024),
        name="spectral",
    )(side, coef, held, turn, matrix, filt, other)


def rotate(value, numerator, denominator):
    numerator = numerator % denominator
    real, imag = value
    if numerator == 0:
        return value
    if 4 * numerator == denominator:
        return (-imag, real)
    angle = 2.0 * math.pi * numerator / denominator
    cos, sin = math.cos(angle), math.sin(angle)
    return (real * cos - imag * sin, real * sin + imag * cos)


def butterflies(values):
    count = len(values)
    if count == 1:
        return values
    even, odd = butterflies(values[0::2]), butterflies(values[1::2])
    out = [None] * count
    for k in range(count // 2):
        turned = rotate(odd[k], k, count)
        out[k] = (even[k][0] + turned[0], even[k][1] + turned[1])
        out[k + count // 2] = (even[k][0] - turned[0], even[k][1] - turned[1])
    return out


def finish_kernel(pair, pieces, gates, result):
    shards, _, _, part, lanes = gates.shape
    pairs = shards // 2
    bits = pairs.bit_length() - 1
    ladders = {}
    for e in range(2):
        for v in range(2):
            terms = []
            for q in range(pairs):
                k = mirrored(q, bits)
                terms.append(rotate((pieces[k, v, e, 0], pieces[k, v, e, 1]), q * v, shards))
            ladders[e, v] = butterflies(terms)
    for i in range(shards):
        plain = ladders[0, i % 2][i // 2]
        odd = rotate(ladders[1, i % 2][i // 2], i, 2 * shards)
        conv = plain[0] + odd[0]
        back = plain[1] + odd[1]
        value = gates[i, 0, 0].astype(jnp.float32)
        gate_in = gates[i, 0, 1].astype(jnp.float32)
        gate_out = gates[i, 0, 2].astype(jnp.float32)
        incoming = gates[i, 0, 3].astype(jnp.float32)
        result[i, 0, 0] = (gate_out * conv).astype(jnp.bfloat16)
        result[i, 0, 1] = (back * gate_in).astype(jnp.bfloat16)
        result[i, 0, 2] = (back * value).astype(jnp.bfloat16)
        result[i, 0, 3] = (incoming * conv).astype(jnp.bfloat16)


def finish(pair, pieces, held):
    shards, groups, _, rows, lanes = held.shape
    part = rows * 2 // shards
    block = (shards, 1, 4, part, lanes)
    return pl.pallas_call(
        finish_kernel,
        grid_spec=pltpu.PrefetchScalarGridSpec(
            num_scalar_prefetch=1,
            grid=(groups,),
            in_specs=[
                pl.BlockSpec((shards // 2, 2, 2, 2, part, lanes), lambda n, k: (0, 0, 0, 0, n, 0)),
                pl.BlockSpec(block, lambda n, k: (0, n, 0, k[0], 0)),
            ],
            out_specs=pl.BlockSpec(block, lambda n, k: (0, n, 0, 0, 0)),
        ),
        out_shape=jax.ShapeDtypeStruct((shards, groups, 4, part, lanes), jnp.bfloat16),
        name="finish",
    )(pair[None], pieces, held)


def transform_matrix(length):
    counter = np.arange(length)
    angle = 2.0 * math.pi * (np.outer(counter, counter) % length) / length
    out = []
    for table in (np.cos(angle), np.sin(angle)):
        high = table.astype(jnp.bfloat16)
        out += [high, (table - high.astype(np.float64)).astype(jnp.bfloat16)]
    return jnp.asarray(np.stack(out))


def on_device(shards, groups, values_in, gate_in, gate_out, cotangent, filter_spectra):
    rows = values_in.shape[0]
    length = rows * groups
    total = 2 * length * shards
    index = lax.axis_index("seq")
    side = index % 2
    own = 2 * mirrored(index, shards.bit_length() - 1) + jnp.arange(2, dtype=jnp.int32)
    shard = jnp.arange(shards, dtype=jnp.int32)
    angle = (2.0 * math.pi / (2 * shards)) * (own[:, None] * shard[None, :] % (2 * shards)).astype(
        jnp.float32
    )
    coef = jnp.stack([jnp.cos(angle), -jnp.sin(angle)], axis=1).reshape(4, shards)
    position = jnp.arange(length, dtype=jnp.int32)
    residue = jnp.stack([own, (own + shards) % (2 * shards)], axis=1)
    angle = (2.0 * math.pi / total) * (residue[..., None] * position % total).astype(jnp.float32)
    turn = jnp.stack([jnp.cos(angle), jnp.sin(angle)], axis=2).reshape(2, 4, length)
    turn = jnp.concatenate([turn, jnp.zeros_like(turn)], axis=1)

    source = arrange((values_in, gate_in, gate_out, cotangent), groups)
    held, other = gather(source, filter_spectra, shards)
    mine, away, packed = spectral(
        side[None], coef, held, turn, transform_matrix(length), filter_spectra, other
    )
    pieces, theirs = trade(packed, away)
    outs = deliver(finish(index // 2, pieces, held))
    grad_filter = jnp.concatenate(
        [jnp.where(side == 0, mine, theirs), jnp.where(side == 0, theirs, mine)], axis=-1
    )
    return (outs[0], outs[1], outs[2], outs[3], grad_filter)


def solution(mesh):
    tokens = P(("seq", "chan"), None)
    spectrum = P(None, "seq", None, None, "chan")
    return jax.shard_map(
        functools.partial(on_device, mesh.shape["seq"], mesh.shape["chan"]),
        mesh=mesh,
        in_specs=(tokens, tokens, tokens, tokens, spectrum),
        out_specs=(tokens, tokens, tokens, tokens, spectrum),
        check_vma=False,
    )
```
